512 devices in a mesh: row: 4 (over x), col: 16 (over z), ch: 8 (over y, core).
Axes of the slice: x: 4, y: 4, z: 16, core: 2. Of those that a mesh axis runs over, the one named last changes fastest.
Arguments:
- features: bfloat16 [192, 256, 2048], P('ch', 'row', 'col'), may hold values from -6 to 6
- cotangent: bfloat16 [192, 256, 2048], P('ch', 'row', 'col'), may hold values from -8 to 8
- dw_kernel: float32 [192, 49], P('ch'), may hold values from -0.875 to 0.875
- dw_bias: float32 [192], P('ch'), may hold values from -1 to 1
- ln_gain: float32 [192], replicated, may hold values from 0.1 to 1.9
- ln_bias: float32 [192], replicated, may hold values from -3 to 3
- w_in: bfloat16 [192, 768], replicated, may hold values from -0.4375 to 0.4375
- in_bias: float32 [768], replicated, may hold values from -3 to 3
- w_out: bfloat16 [768, 192], replicated, may hold values from -0.21875 to 0.21875
- out_bias: float32 [192], replicated, may hold values from -3 to 3
- layer_scale: float32 [192], replicated, may hold values from 0.5 to 2
Outputs:
- output: bfloat16 [192, 256, 2048], P('ch', 'row', 'col')
- grad_input: bfloat16 [192, 256, 2048], P('ch', 'row', 'col')
- grad_w_in: float32 [192, 768], P(None, 'ch')
- grad_w_out: float32 [768, 192], P('ch')
- grad_in_bias: float32 [768], P('ch')
- grad_vectors: float32 [4, 192], replicated
- grad_conv: float32 [192, 50], P('ch')
The draws below stay inside these ranges and needn't reach their ends.
All inputs are finite; a program needn't handle non-finite values.
Results may differ from the reference program's by a relative error of at most 0.015.
Values may be sent and summed in bfloat16 or wider, within the bound.
A program may use at most 64 MiB of HBM per device.

```python
import math
import jax
import jax.numpy as jnp
from jax import lax

C = 192
HID = 768
KW = 7
H = 256
W = 2048


def draw_cotangent(key, part):
    first = jax.random.fold_in(key, 0)
    row_pos = jnp.arange(H, dtype=jnp.float32) / H
    col_pos = jnp.arange(W, dtype=jnp.float32) / W
    spread = 0.6 * jnp.exp(math.log(3.0) * (row_pos[:, None] + col_pos[None, :]))
    noise = jax.random.normal(first, (C, H, W), jnp.float32)
    return jnp.clip(noise * spread[None, :, :], -8.0, 8.0).astype(jnp.bfloat16)


def shard_levels(own_key, shape, cuts, low, largest):
    level = 1.0
    for axis_at, parts in cuts:
        steps = jax.random.uniform(jax.random.fold_in(jax.random.fold_in(own_key, 6), axis_at), (parts,), jnp.float32, low / len(cuts), largest / len(cuts))
        level = level * jnp.repeat(jnp.exp(steps), shape[axis_at] // parts).reshape((-1,) + (1,) * (len(shape) - 1 - axis_at))
    return level


def scatter_about(key, shape, scale, bound, pieces=(), kind=jnp.bfloat16):
    values = jax.random.normal(key, shape, jnp.float32) * scale
    if len(pieces) > 0:
        values = shard_levels(key, shape, pieces, -0.22, 0.18) * values
    return jnp.clip(values, min=-bound, max=bound).astype(kind)


def setup_inputs(seed: int = 0) -> dict:
    seeds = jax.random.split(jax.random.key(seed), 12)
    return {
        "features": scatter_about(seeds[0], (C, H, W), 1.0, 6.0, ((0, 8), (1, 4), (2, 16))),
        "cotangent": draw_cotangent(jax.random.fold_in(seeds[11], 71), 0),
        "dw_kernel": scatter_about(seeds[2], (C, KW * KW), (KW * KW) ** -0.5, 0.875, ((0, 8),), jnp.float32),
        "dw_bias": jnp.clip(jax.random.uniform(seeds[3], (C,), jnp.float32, -1.0, 1.0) * shard_levels(seeds[3], (C,), ((0, 8),), -0.4, 0.0), -1.0, 1.0),
        "ln_gain": jnp.clip(1.0 + 0.18 * jax.random.normal(seeds[4], (C,), jnp.float32), 0.1, 1.9),
        "ln_bias": scatter_about(seeds[5], (C,), 0.5, 3.0, (), jnp.float32),
        "w_in": scatter_about(seeds[6], (C, HID), C ** -0.5, 0.4375),
        "in_bias": scatter_about(seeds[7], (HID,), 0.5, 3.0, (), jnp.float32),
        "w_out": scatter_about(seeds[8], (HID, C), HID ** -0.5, 0.21875),
        "out_bias": scatter_about(seeds[9], (C,), 0.5, 3.0, (), jnp.float32),
        "layer_scale": jnp.clip(jnp.exp(jax.random.uniform(seeds[10], (C,), jnp.float32, math.log(0.5), math.log(2.0))), 0.5, 2.0),
    }


SQRT_HALF = 0.7071067811865476
INV_SQRT_TWO_PI = 0.3989422804014327
EPSILON = 1e-06

def gelu_parts(values):
    cumul = 0.5 * (1.0 + jax.scipy.special.erf(values * SQRT_HALF))
    return (values * cumul, cumul + values * INV_SQRT_TWO_PI * jnp.exp(-0.5 * values * values))

def contract_first(left, right):
    return lax.dot_general(left, right, (((0,), (0,)), ((), ())), preferred_element_type=jnp.float32)

def contract_last(left, right):
    return lax.dot_general(left, right, (((1,), (1,)), ((), ())), preferred_element_type=jnp.float32)

def pointwise_pass(mixed, cotan, ln_gain, ln_bias, w_in, in_bias, w_out, out_bias, layer_scale):
    values = mixed.astype(jnp.float32)
    centre = lax.optimization_barrier(jnp.mean(values, axis=0))
    shifted = values - centre
    inv_std = lax.rsqrt(lax.optimization_barrier(jnp.mean(shifted * shifted, axis=0)) + EPSILON)
    normed = shifted * inv_std
    scaled = (normed * ln_gain[:, None] + ln_bias[:, None]).astype(jnp.bfloat16)
    hidden_pre = contract_first(w_in, scaled) + in_bias[:, None]
    active, slope = gelu_parts(hidden_pre)
    hidden = active.astype(jnp.bfloat16)
    projected = contract_first(w_out, hidden) + out_bias[:, None]
    branch = (layer_scale[:, None] * projected).astype(jnp.bfloat16)
    cot_float = cotan.astype(jnp.float32)
    cot_scaled = (layer_scale[:, None] * cot_float).astype(jnp.bfloat16)
    grad_scale = lax.optimization_barrier(jnp.sum(cot_float * projected, axis=1))
    grad_out_bias = lax.optimization_barrier(jnp.sum(cot_scaled.astype(jnp.float32), axis=1))
    grad_w_out = contract_last(hidden, cot_scaled)
    grad_hidden = (jnp.dot(w_out, cot_scaled, preferred_element_type=jnp.float32) * slope).astype(jnp.bfloat16)
    grad_in_bias = lax.optimization_barrier(jnp.sum(grad_hidden.astype(jnp.float32), axis=1))
    grad_w_in = contract_last(scaled, grad_hidden)
    grad_scaled = jnp.dot(w_in, grad_hidden, preferred_element_type=jnp.float32)
    grad_gain = lax.optimization_barrier(jnp.sum(grad_scaled * normed, axis=1))
    grad_shift = lax.optimization_barrier(jnp.sum(grad_scaled, axis=1))
    grad_normed = grad_scaled * ln_gain[:, None]
    grad_mixed = ((grad_normed - lax.optimization_barrier(jnp.mean(grad_normed, axis=0)) - normed * lax.optimization_barrier(jnp.mean(grad_normed * normed, axis=0))) * inv_std).astype(jnp.bfloat16)
    vectors = jnp.stack([grad_out_bias, grad_gain, grad_shift, grad_scale])
    return (branch, grad_mixed, grad_w_in, grad_w_out, grad_in_bias, vectors)

def depthwise_one(plane, kernel, bias):
    half = KW // 2
    rows, cols = plane.shape
    padded = jnp.pad(plane.astype(jnp.float32), half)
    total = jnp.zeros((rows, cols), jnp.float32) + bias
    for tap_row in range(KW):
        for tap_col in range(KW):
            total = total + kernel[tap_row * KW + tap_col] * padded[tap_row:tap_row + rows, tap_col:tap_col + cols]
    return total.astype(jnp.bfloat16)

def conv_back_one(grad_plane, plane, cot_plane, kernel):
    half = KW // 2
    reach = 2 * half
    rows, cols = plane.shape
    grad_float = grad_plane.astype(jnp.float32)
    grad_pad = jnp.pad(grad_float, half)
    input_pad = jnp.pad(plane.astype(jnp.float32), half)
    result = cot_plane.astype(jnp.float32)
    taps = []
    for tap_row in range(KW):
        for tap_col in range(KW):
            result = result + kernel[tap_row * KW + tap_col] * grad_pad[reach - tap_row:reach - tap_row + rows, reach - tap_col:reach - tap_col + cols]
            taps.append(jnp.sum(grad_float * input_pad[tap_row:tap_row + rows, tap_col:tap_col + cols]))
    taps.append(jnp.sum(grad_float))
    return (result.astype(jnp.bfloat16), jnp.stack(taps))

def reference(features, cotangent, dw_kernel, dw_bias, ln_gain, ln_bias, w_in, in_bias, w_out, out_bias, layer_scale):
    mixed = lax.map(lambda items: depthwise_one(items[0], items[1], items[2]), (features, dw_kernel, dw_bias))
    channels = features.shape[0]
    hidden_units = w_in.shape[1]

    def step(carry, rows):
        branch, grad_mixed, grad_w_in, grad_w_out, grad_in_bias, vectors = pointwise_pass(rows[0], rows[1], ln_gain, ln_bias, w_in, in_bias, w_out, out_bias, layer_scale)
        carry = (carry[0] + grad_w_in, carry[1] + grad_w_out, carry[2] + grad_in_bias, carry[3] + vectors)
        return (carry, (branch, grad_mixed))
    start = (jnp.zeros((channels, hidden_units), jnp.float32), jnp.zeros((hidden_units, channels), jnp.float32), jnp.zeros((hidden_units,), jnp.float32), jnp.zeros((4, channels), jnp.float32))
    totals, (branch_rows, grad_rows) = lax.scan(step, start, (jnp.moveaxis(mixed, 1, 0), jnp.moveaxis(cotangent, 1, 0)))
    branch = jnp.moveaxis(branch_rows, 0, 1)
    grad_mixed = jnp.moveaxis(grad_rows, 0, 1)
    output = (features.astype(jnp.float32) + branch.astype(jnp.float32)).astype(jnp.bfloat16)
    grad_input, conv_terms = lax.map(lambda items: conv_back_one(items[0], items[1], items[2], items[3]), (grad_mixed, features, cotangent, dw_kernel))
    factor = 1.0 / math.sqrt(H * W)
    return (output, grad_input, totals[0] * factor, totals[1] * factor, totals[2] * factor, totals[3] * factor, conv_terms * factor)
```

```python
import functools
import math

import jax
import jax.numpy as jnp
from jax import lax
from jax.experimental import pallas as pl
from jax.experimental.pallas import tpu as pltpu
from jax.sharding import PartitionSpec as P

KW = 7
HALF = 3
LANES = 128
SQRT_HALF = 0.7071067811865476
INV_SQRT_TWO_PI = 0.3989422804014327
EPSILON = 1e-06
MESH = pl.DeviceIdType.MESH
F32 = jnp.float32
BF16 = jnp.bfloat16

ERF_P = 0.3275911 * SQRT_HALF
ERF_A = (0.254829592, -0.284496736, 1.421413741, -1.453152027, 1.061405429)


def gelu_parts(v):
    bell = jnp.exp(-0.5 * v * v)
    t = 1.0 / (1.0 + ERF_P * jnp.abs(v))
    poly = 0.5 * ERF_A[4]
    for a in ERF_A[3::-1]:
        poly = poly * t + 0.5 * a
    tail = poly * t * bell
    cumul = jnp.where(v >= 0, 1.0 - tail, tail)
    return v * cumul, cumul + v * (INV_SQRT_TWO_PI * bell)


def dot(a, b):
    return jnp.dot(a, b, preferred_element_type=F32)


def dot_nt(a, b):
    return lax.dot_general(a, b, (((1,), (1,)), ((), ())), preferred_element_type=F32)


def lane_iota(rows):
    return lax.broadcasted_iota(jnp.int32, (rows, LANES), 1)


def remote(src, dst, send, recv, **where):
    return pltpu.make_async_remote_copy(
        src_ref=src, dst_ref=dst, send_sem=send, recv_sem=recv, device_id=where, device_id_type=MESH
    )


def block_kernel(
    dims,
    feat,
    cot,
    dw_kernel,
    dw_bias,
    cols,
    in_bias,
    w_in,
    w_out,
    out,
    gin,
    gw_out,
    v_out,
    t_out,
    xs,
    gs,
    wb,
    cb,
    vecs,
    edge,
    hrow,
    hedge,
    hcorner,
    edge2,
    hrow2,
    hedge2,
    hcorner2,
    stage,
    gb,
    mb,
    rm,
    rc,
    sb,
    rb,
    wa,
    wint,
    woutt,
    g1,
    g2,
    va,
    sx,
    rx,
    sv,
    rvx,
    sy,
    ry,
    svy,
    rvy,
    taps,
    st,
    rt,
    zt,
    rz,
    zs,
    h_s,
    h_r,
    h2_s,
    h2_r,
    c_s,
    c_r,
    m_s,
    m_r,
    e_s,
    e_r,
    x_s,
    x_r,
    vx_s,
    vx_r,
    y_s,
    y_r,
    vy_s,
    vy_r,
    t_s,
    t_r,
    z_s,
    z_r,
    a_s,
    a_r,
    f_s,
    f_r,
    ring,
):
    n_row, n_col, n_ch, cd, rows, chan, hid = dims
    share = rows // n_ch
    chunks = share // 2
    blk = share * cd
    pair = 2 * cd
    hb = hid // n_ch // n_row
    n_gw = hb // 8 * 3
    n_t = n_gw + 2 + cd // 8
    kb = min(256, hid)
    me_r = lax.axis_index("row")
    me_c = lax.axis_index("col")
    me = lax.axis_index("ch")
    up, down = lax.rem(me_r + n_row - 1, n_row), lax.rem(me_r + 1, n_row)
    left, right = lax.rem(me_c + n_col - 1, n_col), lax.rem(me_c + 1, n_col)

    barrier = pltpu.get_barrier_semaphore()
    near = []
    for k in range(1, n_ch):
        near.append(dict(row=me_r, col=me_c, ch=lax.rem(me + k, n_ch)))
    for k in range(1, n_row):
        near.append(dict(row=lax.rem(me_r + k, n_row), col=me_c, ch=me))
    for c in (left, right):
        for r in (me_r, up, down):
            near.append(dict(row=r, col=c, ch=me))
    for where in near:
        pl.semaphore_signal(barrier, inc=1, device_id=where, device_id_type=MESH)

    def pack_edges(src, buf):
        lane = lane_iota(cd)

        def step(t, acc):
            keep = (lane >= 4 * t) & (lane < 4 * t + 4)
            new = []
            for k in range(rows // 32):
                x = src[pl.ds(pl.multiple_of((HALF + 32 * k + t) * cd, 8), cd), :]
                new.append(jnp.where(keep, pltpu.roll(x, 4 * t, 1), acc[2 * k]))
                new.append(
                    jnp.where(keep, pltpu.roll(x, lax.rem(4 * t + 4, LANES), 1), acc[2 * k + 1])
                )
            return tuple(new)

        zero = jnp.zeros((cd, LANES), F32)
        acc = lax.fori_loop(0, 32, step, (zero,) * (2 * (rows // 32)))
        pad = jnp.zeros((edge_pitch - cd, LANES), F32)
        for k in range(rows // 32):
            for side in range(2):
                full = acc[2 * k + side]
                if edge_pitch > cd:
                    full = jnp.concatenate([full, pad], axis=0)
                buf[side, k] = full.astype(BF16)

    edge_pitch = edge.shape[2]
    n_tiles = rows // 32

    def fill_center(src):
        for q in range(n_ch):
            xs[HALF, pl.ds((HALF + q * share) * cd, blk), :] = src[pl.ds(q * blk, blk), :].astype(F32)

    fill_center(feat)
    pack_edges(xs.at[HALF], edge)

    for t in range(KW * KW):
        wb[pl.ds(t * cd, cd), :] = jnp.broadcast_to(dw_kernel[:, t : t + 1], (cd, LANES))
    cb[...] = jnp.broadcast_to(dw_bias[...], (cd, LANES))

    pl.semaphore_wait(barrier, len(near))

    def halo_copies(src, ebuf, rbuf, lbuf, cbuf, ss, rs):
        four = 4 * cd
        last = (rows - 4) * cd
        copies = [
            remote(src.at[pl.ds(0, four), :], rbuf.at[1], ss.at[0], rs.at[0], row=up, col=me_c, ch=me),
            remote(src.at[pl.ds(last, four), :], rbuf.at[0], ss.at[1], rs.at[1], row=down, col=me_c, ch=me),
            remote(ebuf.at[0], lbuf.at[1], ss.at[2], rs.at[2], row=me_r, col=left, ch=me),
            remote(ebuf.at[1], lbuf.at[0], ss.at[3], rs.at[3], row=me_r, col=right, ch=me),
        ]
        copies.append(remote(ebuf.at[0, 0], cbuf.at[1, 1], ss.at[4], rs.at[4], row=up, col=left, ch=me))
        copies.append(remote(ebuf.at[1, 0], cbuf.at[1, 0], ss.at[5], rs.at[5], row=up, col=right, ch=me))
        copies.append(
            remote(ebuf.at[0, n_tiles - 1], cbuf.at[0, 1], ss.at[6], rs.at[6], row=down, col=left, ch=me)
        )
        copies.append(
            remote(ebuf.at[1, n_tiles - 1], cbuf.at[0, 0], ss.at[7], rs.at[7], row=down, col=right, ch=me)
        )
        return copies

    halo1 = halo_copies(feat, edge, hrow, hedge, hcorner, h_s, h_r)
    for copy in halo1:
        copy.start()

    def cot_copy(k):
        q = lax.rem(me + k, n_ch)
        return remote(cot.at[q], rc.at[me], c_s.at[q], c_r.at[me], row=me_r, col=me_c, ch=q)

    def came(buf, ss, rs, q, idx=None):
        dst = buf.at[q] if idx is None else buf.at[q, idx]
        recv = rs.at[q] if idx is None else rs.at[q, idx]
        send = ss.at[q] if idx is None else ss.at[q, idx]
        return remote(dst, dst, send, recv, row=me_r, col=me_c, ch=q)

    for k in range(1, n_ch):
        cot_copy(k).start()

    eye = lambda n: (
        lax.broadcasted_iota(jnp.int32, (n, n), 0) == lax.broadcasted_iota(jnp.int32, (n, n), 1)
    ).astype(BF16)
    wa[pl.ds(0, chan), :] = w_in[...]
    bias_row = in_bias[...]
    hi = bias_row.astype(BF16).astype(F32)
    lo = bias_row - hi
    row_id = lax.broadcasted_iota(jnp.int32, (64, hid), 0)
    wa[pl.ds(chan, 64), :] = jnp.where(
        row_id == 0, jnp.broadcast_to(hi, (64, hid)), jnp.where(row_id == 1, jnp.broadcast_to(lo, (64, hid)), 0.0)
    ).astype(BF16)
    for k in range(hid // kb):
        wint[pl.ds(k * kb, kb), :] = dot_nt(eye(kb), wa[:, k * kb : (k + 1) * kb]).astype(BF16)
        woutt[:, k * kb : (k + 1) * kb] = dot_nt(eye(chan), w_out[pl.ds(k * kb, kb), :]).astype(BF16)
    for k in range(4):
        vecs[k] = jnp.broadcast_to(cols[:, k : k + 1], (chan, LANES))
    g1[...] = jnp.zeros_like(g1)
    g2[...] = jnp.zeros_like(g2)
    va[...] = jnp.zeros_like(va)
    taps[...] = jnp.zeros_like(taps)
    rc[me] = cot[me]

    def as_f32(flag):
        return jnp.where(flag, 1.0, 0.0).astype(F32)

    def shifted_copies(buf, rbuf, lbuf, cbuf):
        has_up, has_down = as_f32(me_r > 0), as_f32(me_r < n_row - 1)
        has_left, has_right = as_f32(me_c > 0), as_f32(me_c < n_col - 1)
        buf[HALF, pl.ds(0, HALF * cd), :] = rbuf[0].astype(F32)[cd:] * has_up
        buf[HALF, pl.ds((HALF + rows) * cd, HALF * cd), :] = rbuf[1].astype(F32)[: HALF * cd] * has_down
        for side, has in ((0, has_left), (1, has_right)):
            stage[side, 0] = cbuf[0, side].astype(F32)[:cd] * (has * has_up)
            for k in range(n_tiles):
                stage[side, 1 + k] = lbuf[side, k].astype(F32)[:cd] * has
            stage[side, 1 + n_tiles] = cbuf[1, side].astype(F32)[:cd] * (has * has_down)
        lane = lane_iota(cd)

        def one_row(i, carry):
            at = i + 32 - HALF
            tile, t = lax.div(at, 32), lax.rem(at, 32)
            halo = jnp.where(
                lane < 64,
                pltpu.roll(stage[1, tile], lax.rem(LANES - 4 * t, LANES), 1),
                pltpu.roll(stage[0, tile], 124 - 4 * t, 1),
            )
            where = pl.ds(pl.multiple_of(i * cd, 8), cd)
            x = buf[HALF, where, :]
            for s in range(1, HALF + 1):
                buf[HALF + s, where, :] = pltpu.roll(jnp.where(lane < s, halo, x), LANES - s, 1)
                buf[HALF - s, where, :] = pltpu.roll(jnp.where(lane >= LANES - s, halo, x), s, 1)
            return carry

        lax.fori_loop(0, rows + 2 * HALF, one_row, 0)

    for copy in halo1:
        copy.wait_recv()

    reach = []
    r = 2
    while r < n_col // 2:
        reach.append(r)
        r *= 2

    def tell(i):
        for step in (reach[i], n_col - reach[i]):
            pl.semaphore_signal(
                ring.at[i],
                inc=1,
                device_id=dict(row=me_r, col=lax.rem(me_c + step, n_col), ch=me),
                device_id_type=MESH,
            )

    if reach:
        tell(0)

    shifted_copies(xs, hrow, hedge, hcorner)

    def conv(buf, base, start, flip):
        acc = start
        for b in range(KW):
            for a in range(KW):
                tap = (KW - 1 - a) * KW + KW - 1 - b if flip else a * KW + b
                w = wb[pl.ds(tap * cd, cd), :]
                x = buf[b, pl.ds(pl.multiple_of((base + a) * cd, 8), blk), :]
                acc = acc + jnp.concatenate([w] * share, axis=0) * x
        return acc

    def mix_copy(q):
        return remote(mb.at[q], rm.at[me], m_s.at[q], m_r.at[me], row=me_r, col=me_c, ch=q)

    def forward(k, carry):
        q = lax.rem(me + 1 + k, n_ch)
        start = jnp.concatenate([cb[...]] * share, axis=0)
        mb[q] = conv(xs, q * share, start, False).astype(BF16)

        @pl.when(k < n_ch - 1)
        def _():
            mix_copy(q).start()

        return carry

    lax.fori_loop(0, n_ch, forward, 0)
    rm[me] = mb[me]

    for k in range(1, n_ch):
        q = lax.rem(me + k, n_ch)
        came(rc, c_s, c_r, q).wait_recv()
        came(rm, m_s, m_r, q).wait_recv()

    if len(reach) > 1:
        pl.semaphore_wait(ring.at[0], 2)
        tell(1)

    px = 2 * LANES
    ones_rows = (lax.broadcasted_iota(jnp.int32, (64, px), 0) < 2).astype(F32).astype(BF16)

    def wide(v):
        return jnp.concatenate([v, v], axis=1)

    def gather(buf, at):
        parts = []
        for q in range(n_ch):
            both = buf[q, at, :].astype(F32)
            parts.append(jnp.concatenate([both[:cd], both[cd:]], axis=1))
        return jnp.concatenate(parts, axis=0)

    def exit_copy(q, k):
        return remote(sb.at[q, k], rb.at[me, k], e_s.at[q, k], e_r.at[me, k], row=me_r, col=me_c, ch=q)

    def fold(v):
        return v[:, :LANES] + v[:, LANES:]

    def chunk(k, carry):
        at = pl.ds(pl.multiple_of(k * pair, 16), pair)
        gain, shift, outb, scale = (wide(vecs[i]) for i in range(4))
        values = gather(rm, at)
        centre = jnp.mean(values, axis=0, keepdims=True)
        away = values - centre
        inv_std = lax.rsqrt(jnp.mean(away * away, axis=0, keepdims=True) + EPSILON)
        normed = away * inv_std
        scaled = (normed * gain + shift).astype(BF16)
        scaled = jnp.concatenate([scaled, ones_rows], axis=0)
        cotan = gather(rc, at)
        cots = (cotan * scale).astype(BF16)
        projected = jnp.zeros((chan, px), F32)
        grad_scaled = jnp.zeros((chan, px), F32)
        for j in range(hid // kb):
            rows_j = pl.ds(j * kb, kb)
            act, slope = gelu_parts(dot(wint[rows_j, :], scaled))
            hidden = act.astype(BF16)
            grad_hidden = (dot(w_out[rows_j, :], cots) * slope).astype(BF16)
            projected = projected + dot(woutt[:, j * kb : (j + 1) * kb], hidden)
            grad_scaled = grad_scaled + dot(w_in[:, j * kb : (j + 1) * kb], grad_hidden)
            g1[rows_j, :] += dot_nt(grad_hidden, scaled)
            g2[rows_j, :] += dot_nt(hidden, cots)
        projected = projected + outb
        branch = scale * projected
        va[0] += fold(cots.astype(F32))
        va[1] += fold(grad_scaled * normed)
        va[2] += fold(grad_scaled)
        va[3] += fold(cotan * projected)
        gn = grad_scaled * gain
        m1 = jnp.mean(gn, axis=0, keepdims=True)
        m2 = jnp.mean(gn * normed, axis=0, keepdims=True)
        gm = (gn - m1 - normed * m2) * inv_std
        for q in range(n_ch):
            for i, v in enumerate((branch, gm)):
                piece = v[q * cd : (q + 1) * cd]
                sb[q, k, pl.ds(i * pair, pair), :] = jnp.concatenate(
                    [piece[:, :LANES], piece[:, LANES:]], axis=0
                ).astype(BF16)
        for d in range(1, n_ch):
            exit_copy(lax.rem(me + d, n_ch), k).start()
        rb[me, k] = sb[me, k]
        return carry

    lax.fori_loop(0, chunks, chunk, 0)

    half = lane_iota(pair_rows := 2 * hb) < 64
    for r in range(n_row):
        for q in range(0, n_ch, 2):
            at = [(q + i) * hb * n_row + r * hb for i in range(2)]
            a, b = (
                jnp.concatenate([g[pl.ds(at[i], hb), :] for i in range(2)], axis=0) for g in (g1, g2)
            )
            b_hi = pltpu.roll(
                jnp.concatenate([b[:, LANES:], jnp.zeros((pair_rows, 2 * LANES - chan), F32)], axis=1), 64, 1
            )
            sx[r, pl.ds(q * hb, pair_rows), :] = jnp.concatenate(
                [a[:, :LANES], b[:, :LANES], jnp.where(half, a[:, LANES:], b_hi)], axis=1
            ).astype(BF16)
    lane_c = lane_iota(chan)
    table = jnp.zeros((chan, LANES), F32)
    for i in range(4):
        table = jnp.where(lane_c == i, jnp.sum(va[i], axis=1, keepdims=True), table)
    for i in range(hid // chan):
        part = pltpu.roll(g1[pl.ds(i * chan, chan), LANES:], LANES - 64 + 4 + i, 1)
        table = jnp.where(lane_c == 4 + i, part, table)
    table = jnp.concatenate([table, jnp.zeros((2 * LANES - chan, LANES), F32)], axis=0)
    sv[...] = table.T[:8]

    def x_copies(k):
        r = lax.rem(me_r + k, n_row)
        return (
            remote(sx.at[r], rx.at[me_r], x_s.at[r], x_r.at[me_r], row=r, col=me_c, ch=me),
            remote(sv, rvx.at[me_r], vx_s.at[r], vx_r.at[me_r], row=r, col=me_c, ch=me),
        )

    for k in range(1, n_row):
        for copy in x_copies(k):
            copy.start()
    rx[me_r] = sx[me_r]
    rvx[me_r] = sv[...]

    for d in range(1, n_ch):
        q = lax.rem(me + d, n_ch)
        for k in range(chunks):
            came(rb, e_s, e_r, q, k).wait_recv()

    def unpack(q, carry):
        for k in range(chunks):
            at = q * blk + k * pair
            grad = rb[q, k, pl.ds(pair, pair), :]
            gb[pl.ds(pl.multiple_of(at, 16), pair), :] = grad
            gs[HALF, pl.ds(pl.multiple_of(HALF * cd + at, 8), pair), :] = grad.astype(F32)
        return carry

    lax.fori_loop(0, n_ch, unpack, 0)
    pack_edges(gs.at[HALF], edge2)
    halo2 = halo_copies(gb, edge2, hrow2, hedge2, hcorner2, h2_s, h2_r)
    for copy in halo2:
        copy.start()

    def add_rows(v):
        total = v[:cd]
        for i in range(1, share):
            total = total + v[i * cd : (i + 1) * cd]
        return total

    def tap_block(q, carry):
        g = gs[HALF, pl.ds(pl.multiple_of((HALF + q * share) * cd, 8), blk), :]
        for b in range(KW):
            for a in range(KW):
                x = xs[b, pl.ds(pl.multiple_of((q * share + a) * cd, 8), blk), :]
                taps[pl.ds((a * KW + b) * cd, cd), :] += add_rows(g * x)
        taps[pl.ds(KW * KW * cd, cd), :] += add_rows(g)
        return carry

    lax.fori_loop(0, n_ch // 2, tap_block, 0)

    for k in range(1, n_row):
        r = lax.rem(me_r + k, n_row)
        remote(rx.at[r], rx.at[r], x_s.at[r], x_r.at[r], row=r, col=me_c, ch=me).wait_recv()
        remote(rvx.at[r], rvx.at[r], vx_s.at[r], vx_r.at[r], row=r, col=me_c, ch=me).wait_recv()
    for q in range(0, n_ch, 2):
        at = pl.ds(q * hb, 2 * hb)
        total = rx[0, at, :].astype(F32)
        for r in range(1, n_row):
            total = total + rx[r, at, :].astype(F32)
        sy[q] = total[:hb]
        sy[q + 1] = total[hb:]
    total = rvx[0]
    for r in range(1, n_row):
        total = total + rvx[r]
    svy[...] = total

    def y_copies(k):
        q = lax.rem(me + k, n_ch)
        return (
            remote(sy.at[q], ry.at[me], y_s.at[q], y_r.at[me], row=me_r, col=me_c, ch=q),
            remote(svy, rvy.at[me], vy_s.at[q], vy_r.at[me], row=me_r, col=me_c, ch=q),
        )

    for k in range(1, n_ch):
        for copy in y_copies(k):
            copy.start()
    ry[me] = sy[me]
    rvy[me] = svy[...]

    lax.fori_loop(n_ch // 2, n_ch, tap_block, 0)
    lane_d = lane_iota(cd)

    def tap_sum(t, acc):
        col = jnp.sum(taps[pl.ds(pl.multiple_of(t * cd, 8), cd), :], axis=1, keepdims=True)
        return jnp.where(lane_d == t, col, acc)

    st[...] = lax.fori_loop(0, KW * KW + 1, tap_sum, jnp.zeros((cd, LANES), F32))

    def t_copy(k):
        r = lax.rem(me_r + k, n_row)
        return remote(st, rt.at[me_r], t_s.at[r], t_r.at[me_r], row=r, col=me_c, ch=me)

    for k in range(1, n_row):
        t_copy(k).start()
    rt[me_r] = st[...]

    for k in range(1, n_ch):
        q = lax.rem(me + k, n_ch)
        came(ry, y_s, y_r, q).wait_recv()
        came(rvy, vy_s, vy_r, q).wait_recv()
    total, vtotal = ry[0], rvy[0]
    for q in range(1, n_ch):
        total = total + ry[q]
        vtotal = vtotal + rvy[q]
    for i in range(hb // 8):
        for j in range(3):
            zt[3 * i + j] = total[8 * i : 8 * i + 8, j * LANES : (j + 1) * LANES]
    zt[n_gw] = vtotal[:, :LANES]
    zt[n_gw + 1] = vtotal[:, LANES:]
    for k in range(1, n_row):
        r = lax.rem(me_r + k, n_row)
        remote(rt.at[r], rt.at[r], t_s.at[r], t_r.at[r], row=r, col=me_c, ch=me).wait_recv()
    ttotal = rt[0]
    for r in range(1, n_row):
        ttotal = ttotal + rt[r]
    for i in range(cd // 8):
        zt[n_gw + 2 + i] = ttotal[8 * i : 8 * i + 8]

    for i in range(len(reach)):
        if i == len(reach) - 1:
            pl.semaphore_wait(ring.at[i], 2)

    def z_copy(t):
        owner = lax.rem(t, n_col)
        return remote(zt.at[t], rz.at[t, me_c], z_s.at[t], z_r.at[t, me_c], row=me_r, col=owner, ch=me)

    def z_send(t, carry):
        mine = lax.rem(t, n_col) == me_c

        @pl.when(jnp.logical_not(mine))
        def _():
            z_copy(t).start()

        @pl.when(mine)
        def _():
            rz[t, me_c] = zt[t]

        return carry

    lax.fori_loop(0, n_t, z_send, 0)

    for copy in halo2:
        copy.wait_recv()
    shifted_copies(gs, hrow2, hedge2, hcorner2)

    def backward(q, carry):
        start = cot[q].astype(F32)
        rows_q = pl.ds(pl.multiple_of(q * blk, 16), blk)
        gin[rows_q, :] = conv(gs, q * share, start, True).astype(BF16)
        for k in range(chunks):
            at = pl.ds(pl.multiple_of(q * blk + k * pair, 16), pair)
            out[at, :] = (feat[at, :].astype(F32) + rb[q, k, pl.ds(0, pair), :].astype(F32)).astype(BF16)
        return carry

    lax.fori_loop(0, n_ch, backward, 0)

    def a_copy(t, c):
        return remote(zs.at[t], zs.at[t], a_s.at[t, c], a_r.at[t], row=me_r, col=c, ch=me)

    def z_own(t, carry):
        @pl.when(lax.rem(t, n_col) == me_c)
        def _():
            def one(d, c2):
                c = lax.rem(me_c + d, n_col)
                remote(rz.at[t, c], rz.at[t, c], z_s.at[t], z_r.at[t, c], row=me_r, col=c, ch=me).wait_recv()
                return c2

            lax.fori_loop(1, n_col, one, 0)
            total = rz[t, 0]
            for c in range(1, n_col):
                total = total + rz[t, c]
            zs[t] = total

            def give(d, c2):
                a_copy(t, lax.rem(me_c + d, n_col)).start()
                return c2

            lax.fori_loop(1, n_col, give, 0)

        return carry

    lax.fori_loop(0, n_t, z_own, 0)

    def z_arrived(t, carry):
        @pl.when(lax.rem(t, n_col) != me_c)
        def _():
            a_copy(t, lax.rem(t, n_col)).wait_recv()

        return carry

    lax.fori_loop(0, n_t, z_arrived, 0)

    gw = zs.at[pl.ds(0, n_gw)]

    def f_copy(k):
        r = lax.rem(me_r + k, n_row)
        return remote(gw, gw_out.at[me_r], f_s.at[r], f_r.at[me_r], row=r, col=me_c, ch=me)

    for k in range(1, n_row):
        f_copy(k).start()
    gw_out[me_r] = zs[pl.ds(0, n_gw)]
    for j in range(2):
        v_out[:, j * LANES : (j + 1) * LANES] = zs[n_gw + j]
    for i in range(cd // 8):
        t_out[pl.ds(8 * i, 8), :] = zs[n_gw + 2 + i]

    for copy in halo1 + halo2:
        copy.wait_send()
    for k in range(1, n_ch):
        cot_copy(k).wait_send()
        q = lax.rem(me + k, n_ch)
        mix_copy(q).wait_send()
        for j in range(chunks):
            exit_copy(q, j).wait_send()
        for copy in y_copies(k):
            copy.wait_send()
    for k in range(1, n_row):
        for copy in x_copies(k):
            copy.wait_send()
        t_copy(k).wait_send()

    def z_drain(t, carry):
        mine = lax.rem(t, n_col) == me_c

        @pl.when(jnp.logical_not(mine))
        def _():
            z_copy(t).wait_send()

        @pl.when(mine)
        def _():
            def one(d, c2):
                a_copy(t, lax.rem(me_c + d, n_col)).wait_send()
                return c2

            lax.fori_loop(1, n_col, one, 0)

        return carry

    lax.fori_loop(0, n_t, z_drain, 0)
    for k in range(1, n_row):
        r = lax.rem(me_r + k, n_row)
        remote(gw_out.at[r], gw_out.at[r], f_s.at[r], f_r.at[r], row=r, col=me_c, ch=me).wait_recv()
        f_copy(k).wait_send()


def run_block(dims, feat, cot, dw_kernel, dw_bias, cols, in_bias, w_in, w_out):
    n_row, n_col, n_ch, cd, rows, chan, hid = dims
    share = rows // n_ch
    chunks = share // 2
    blk = share * cd
    hb = hid // n_ch // n_row
    n_gw = hb // 8 * 3
    n_t = n_gw + 2 + cd // 8
    pitch = -(-cd // 16) * 16
    n_tiles = rows // 32
    lanes_w = 3 * LANES
    padded = (rows + 2 * HALF) * cd
    vmem = lambda *shape: pltpu.VMEM(shape[:-1], shape[-1])
    dma = lambda *shape: pltpu.SemaphoreType.DMA(shape)
    halo_bufs = [
        vmem(2, n_tiles, pitch, LANES, BF16),
        vmem(2, 4 * cd, LANES, BF16),
        vmem(2, n_tiles, pitch, LANES, BF16),
        vmem(2, 2, pitch, LANES, BF16),
    ]
    scratch = [
        vmem(KW, padded, LANES, F32),
        vmem(KW, padded, LANES, F32),
        vmem(KW * KW * cd, LANES, F32),
        vmem(cd, LANES, F32),
        vmem(4, chan, LANES, F32),
        *halo_bufs,
        *halo_bufs,
        vmem(2, n_tiles + 2, cd, LANES, F32),
        vmem(rows * cd, LANES, BF16),
        vmem(n_ch, blk, LANES, BF16),
        vmem(n_ch, blk, LANES, BF16),
        vmem(n_ch, blk, LANES, BF16),
        vmem(n_ch, chunks, 4 * cd, LANES, BF16),
        vmem(n_ch, chunks, 4 * cd, LANES, BF16),
        vmem(chan + 64, hid, BF16),
        vmem(hid, chan + 64, BF16),
        vmem(chan, hid, BF16),
        vmem(hid, chan + 64, F32),
        vmem(hid, chan, F32),
        vmem(4, chan, LANES, F32),
        vmem(n_row, n_ch * hb, lanes_w, BF16),
        vmem(n_row, n_ch * hb, lanes_w, BF16),
        vmem(8, 2 * LANES, F32),
        vmem(n_row, 8, 2 * LANES, F32),
        vmem(n_ch, hb, lanes_w, F32),
        vmem(n_ch, hb, lanes_w, F32),
        vmem(8, 2 * LANES, F32),
        vmem(n_ch, 8, 2 * LANES, F32),
        vmem((KW * KW + 1) * cd, LANES, F32),
        vmem(cd, LANES, F32),
        vmem(n_row, cd, LANES, F32),
        vmem(n_t, 8, LANES, F32),
        vmem(n_t, n_col, 8, LANES, F32),
        vmem(n_t, 8, LANES, F32),
        dma(8), dma(8),
        dma(8), dma(8),
        dma(n_ch), dma(n_ch),
        dma(n_ch), dma(n_ch),
        dma(n_ch, chunks), dma(n_ch, chunks),
        dma(n_row), dma(n_row),
        dma(n_row), dma(n_row),
        dma(n_ch), dma(n_ch),
        dma(n_ch), dma(n_ch),
        dma(n_row), dma(n_row),
        dma(n_t), dma(n_t, n_col),
        dma(n_t, n_col), dma(n_t),
        dma(n_row), dma(n_row),
        pltpu.SemaphoreType.REGULAR((4,)),
    ]
    whole = pl.BlockSpec(memory_space=pltpu.VMEM)
    return pl.pallas_call(
        functools.partial(block_kernel, dims),
        name="convnext_block",
        out_shape=(
            jax.ShapeDtypeStruct((rows * cd, LANES), BF16),
            jax.ShapeDtypeStruct((rows * cd, LANES), BF16),
            jax.ShapeDtypeStruct((n_row, n_gw, 8, LANES), F32),
            jax.ShapeDtypeStruct((8, 2 * LANES), F32),
            jax.ShapeDtypeStruct((cd, LANES), F32),
        ),
        in_specs=[whole] * 8,
        out_specs=(whole,) * 5,
        scratch_shapes=scratch,
        compiler_params=pltpu.CompilerParams(
            collective_id=0, has_side_effects=True, vmem_limit_bytes=56 * 1024 * 1024
        ),
    )(feat, cot, dw_kernel, dw_bias, cols, in_bias, w_in, w_out)


def body(
    n_row,
    n_col,
    n_ch,
    features,
    cotangent,
    dw_kernel,
    dw_bias,
    ln_gain,
    ln_bias,
    w_in,
    in_bias,
    w_out,
    out_bias,
    layer_scale,
):
    cd, rows, wide = features.shape
    chan, hid = w_in.shape
    dims = (n_row, n_col, n_ch, cd, rows, chan, hid)
    feat = features.transpose(1, 0, 2).reshape(rows * cd, wide)
    cot = cotangent.transpose(1, 0, 2).reshape(n_ch, rows // n_ch * cd, wide)
    cols = jnp.stack([ln_gain, ln_bias, out_bias, layer_scale], axis=1)
    out, gin, gw, vecs, taps = run_block(
        dims, feat, cot, dw_kernel, dw_bias[:, None], cols, in_bias[None], w_in, w_out
    )
    back = lambda v: v.reshape(rows, cd, wide).transpose(1, 0, 2)
    factor = 1.0 / math.sqrt(rows * n_row * wide * n_col)
    hs = hid // n_ch
    gw = gw.reshape(n_row, hs // n_row // 8, 3, 8, LANES).transpose(0, 1, 3, 2, 4).reshape(hs, 3 * LANES)
    gw = gw * factor
    rest = chan - LANES
    g_in = jnp.concatenate([gw[:, :LANES], gw[:, 2 * LANES : 2 * LANES + rest]], axis=1).T
    g_out = jnp.concatenate([gw[:, LANES : 2 * LANES], gw[:, 2 * LANES + 64 : 2 * LANES + 64 + rest]], axis=1)
    vecs = vecs[:, :chan] * factor
    bias = lax.dynamic_slice_in_dim(vecs[4:].reshape(-1), lax.axis_index("ch") * hs, hs, 0)
    return (
        back(out),
        back(gin),
        g_in,
        g_out,
        bias,
        vecs[:4],
        taps[:, : KW * KW + 1] * factor,
    )


def solution(mesh):
    ch = P("ch", "row", "col")
    in_specs = (ch, ch, P("ch", None), P("ch")) + (P(),) * 7
    out_specs = (ch, ch, P(None, "ch"), P("ch", None), P("ch"), P(), P("ch", None))
    sizes = (mesh.shape["row"], mesh.shape["col"], mesh.shape["ch"])
    return jax.shard_map(
        functools.partial(body, *sizes), mesh=mesh, in_specs=in_specs, out_specs=out_specs, check_vma=False
    )
```

```python
import functools
import math

import jax
import jax.numpy as jnp
from jax import lax
from jax.experimental import pallas as pl
from jax.experimental.pallas import tpu as pltpu
from jax.sharding import PartitionSpec as P

KW = 7
HALF = 3
LANES = 128
SQRT_HALF = 0.7071067811865476
INV_SQRT_TWO_PI = 0.3989422804014327
EPSILON = 1e-06
MESH = pl.DeviceIdType.MESH
F32 = jnp.float32
BF16 = jnp.bfloat16

ERF_P = 0.3275911 * SQRT_HALF
ERF_A = (0.254829592, -0.284496736, 1.421413741, -1.453152027, 1.061405429)


def gelu_parts(v):
    bell = jnp.exp2((-0.5 * math.log2(math.e)) * (v * v))
    t = 1.0 / (1.0 + ERF_P * jnp.abs(v))
    poly = 0.5 * ERF_A[4]
    for a in ERF_A[3::-1]:
        poly = poly * t + 0.5 * a
    tail = poly * t * bell
    cumul = jnp.where(v >= 0, 1.0 - tail, tail)
    return v * cumul, cumul + v * (INV_SQRT_TWO_PI * bell)


def dot(a, b):
    return jnp.dot(a, b, preferred_element_type=F32)


def dot_nt(a, b):
    return lax.dot_general(a, b, (((1,), (1,)), ((), ())), preferred_element_type=F32)


def lane_iota(rows):
    return lax.broadcasted_iota(jnp.int32, (rows, LANES), 1)


def remote(src, dst, send, recv, **where):
    return pltpu.make_async_remote_copy(
        src_ref=src, dst_ref=dst, send_sem=send, recv_sem=recv, device_id=where, device_id_type=MESH
    )


def block_kernel(
    dims,
    feat,
    cot,
    dw_kernel,
    dw_bias,
    ln_gain,
    ln_bias,
    out_bias,
    layer_scale,
    in_bias,
    w_in,
    woutt,
    out,
    gin,
    fx,
    v_out,
    plain,
    ca,
    ends,
    ends2,
    xs,
    gs,
    cbuf,
    wb,
    cb,
    vecs,
    edge,
    hrow,
    hedge,
    hcorner,
    edge2,
    hrow2,
    hedge2,
    hcorner2,
    stage,
    mb,
    rm,
    rc,
    sb,
    rb,
    wa,
    wint,
    w_out,
    g1,
    g2,
    va,
    sc,
    rxc,
    sx,
    rx,
    sv,
    rvc,
    svx,
    rvx,
    sy,
    ry,
    svy,
    rvy,
    taps,
    zt,
    rz,
    zs,
    h_s,
    h_r,
    h2_s,
    h2_r,
    c_s,
    c_r,
    m_s,
    m_r,
    e_s,
    e_r,
    p_s,
    p_r,
    x_s,
    x_r,
    vx_s,
    vx_r,
    y_s,
    y_r,
    vy_s,
    vy_r,
    z_s,
    z_r,
    a_s,
    a_r,
    f_s,
    f_r,
    ring,
):
    n_row, n_col, n_ch, cd, rows, chan, hid = dims
    share = rows // n_ch
    chunks = share // 2
    blk = share * cd
    pair = 2 * cd
    hb = hid // n_ch // n_row
    n_gw = hb // 8 * 3
    n_t = n_gw + 2 + cd // 8
    kb = min(256, hid)
    n_y = n_ch // 2
    me_r = lax.axis_index("row")
    me_c = lax.axis_index("col")
    me = lax.axis_index("ch")
    core, me_y = lax.rem(me, 2), lax.div(me, 2)
    mate = me + 1 - 2 * core
    up, down = lax.rem(me_r + n_row - 1, n_row), lax.rem(me_r + 1, n_row)
    left, right = lax.rem(me_c + n_col - 1, n_col), lax.rem(me_c + 1, n_col)

    barrier = pltpu.get_barrier_semaphore()
    near = []
    for k in range(1, n_ch):
        near.append(dict(row=me_r, col=me_c, ch=lax.rem(me + k, n_ch)))
    for k in range(1, n_row):
        near.append(dict(row=lax.rem(me_r + k, n_row), col=me_c, ch=me))
    for c in (left, right):
        for r in (me_r, up, down):
            near.append(dict(row=r, col=c, ch=me))
    for where in near:
        pl.semaphore_signal(barrier, inc=1, device_id=where, device_id_type=MESH)

    edge_pitch = edge.shape[2]
    n_tiles = rows // 32

    def pack_edges(src, buf, row_ends):
        lane = lane_iota(cd)
        acc = [jnp.zeros((cd, LANES), F32)] * (2 * n_tiles)
        for t in range(32):
            keep = (lane >= 4 * t) & (lane < 4 * t + 4)
            for k in range(n_tiles):
                x = src[pl.ds((HALF + 32 * k + t) * cd, cd), :]
                for side, turn in ((0, 4 * t), (1, (4 * t + 4) % LANES)):
                    moved = pltpu.roll(x, turn, 1) if turn else x
                    acc[2 * k + side] = jnp.where(keep, moved, acc[2 * k + side])
        pad = jnp.zeros((edge_pitch - cd, LANES), F32)
        for k in range(n_tiles):
            for side in range(2):
                full = acc[2 * k + side]
                if edge_pitch > cd:
                    full = jnp.concatenate([full, pad], axis=0)
                buf[side, k] = full.astype(BF16)
        row_ends[0] = src[pl.ds(HALF * cd, 4 * cd), :].astype(BF16)
        row_ends[1] = src[pl.ds((HALF + rows - 4) * cd, 4 * cd), :].astype(BF16)

    def by_rows(src):
        for c in range(cd):
            plain[pl.ds(c * rows, rows), :] = src[c].astype(F32)

    def plain_row(i):
        return plain[pl.ds(i, cd, stride=rows), :]

    by_rows(feat)
    for i in range(rows):
        xs[HALF, pl.ds((HALF + i) * cd, cd), :] = plain_row(i)
    pack_edges(xs.at[HALF], edge, ends)

    pl.semaphore_wait(barrier, len(near))

    def halo_copies(src, ebuf, rbuf, lbuf, cbuf, ss, rs):
        copies = [
            remote(src.at[0], rbuf.at[1], ss.at[0], rs.at[0], row=up, col=me_c, ch=me),
            remote(src.at[1], rbuf.at[0], ss.at[1], rs.at[1], row=down, col=me_c, ch=me),
            remote(ebuf.at[0], lbuf.at[1], ss.at[2], rs.at[2], row=me_r, col=left, ch=me),
            remote(ebuf.at[1], lbuf.at[0], ss.at[3], rs.at[3], row=me_r, col=right, ch=me),
        ]
        copies.append(remote(ebuf.at[0, 0], cbuf.at[1, 1], ss.at[4], rs.at[4], row=up, col=left, ch=me))
        copies.append(remote(ebuf.at[1, 0], cbuf.at[1, 0], ss.at[5], rs.at[5], row=up, col=right, ch=me))
        copies.append(
            remote(ebuf.at[0, n_tiles - 1], cbuf.at[0, 1], ss.at[6], rs.at[6], row=down, col=left, ch=me)
        )
        copies.append(
            remote(ebuf.at[1, n_tiles - 1], cbuf.at[0, 0], ss.at[7], rs.at[7], row=down, col=right, ch=me)
        )
        return copies

    halo1 = halo_copies(ends, edge, hrow, hedge, hcorner, h_s, h_r)
    for copy in halo1:
        copy.start()

    def cot_copy(k):
        q = lax.rem(me + k, n_ch)
        return remote(ca.at[q], rc.at[me], c_s.at[q], c_r.at[me], row=me_r, col=me_c, ch=q)

    def came(buf, ss, rs, q, idx=None):
        dst = buf.at[q] if idx is None else buf.at[q, idx]
        recv = rs.at[q] if idx is None else rs.at[q, idx]
        send = ss.at[q] if idx is None else ss.at[q, idx]
        return remote(dst, dst, send, recv, row=me_r, col=me_c, ch=q)

    by_rows(cot)
    for i in range(0, rows, 2):
        ca[i // share, pl.ds(i % share * cd, pair), :] = jnp.concatenate(
            [plain_row(i), plain_row(i + 1)], axis=0
        ).astype(BF16)
    for k in range(1, n_ch):
        cot_copy(k).start()

    for t in range(KW * KW):
        wb[pl.ds(t * cd, cd), :] = jnp.broadcast_to(dw_kernel[:, t : t + 1], (cd, LANES))

    def as_row(ref, width):
        row = ref[...].reshape(1, ref.shape[0])
        if width > ref.shape[0]:
            row = jnp.concatenate([row, jnp.zeros((1, width - ref.shape[0]), F32)], axis=1)
        return row

    wide_rows = [as_row(v, 2 * LANES) for v in (ln_gain, ln_bias, out_bias, layer_scale, dw_bias)]
    table = jnp.concatenate(wide_rows + [jnp.zeros((LANES - 5, 2 * LANES), F32)], axis=0).T
    for k in range(4):
        vecs[k] = jnp.broadcast_to(table[:chan, k : k + 1], (chan, LANES))
    cb[...] = jnp.broadcast_to(table[:cd, 4:5], (cd, LANES))
    eye = lambda n: (
        lax.broadcasted_iota(jnp.int32, (n, n), 0) == lax.broadcasted_iota(jnp.int32, (n, n), 1)
    ).astype(BF16)
    wa[pl.ds(0, chan), :] = w_in[...]
    bias_row = as_row(in_bias, hid)
    hi = bias_row.astype(BF16).astype(F32)
    lo = bias_row - hi
    row_id = lax.broadcasted_iota(jnp.int32, (64, hid), 0)
    wa[pl.ds(chan, 64), :] = jnp.where(
        row_id == 0, jnp.broadcast_to(hi, (64, hid)), jnp.where(row_id == 1, jnp.broadcast_to(lo, (64, hid)), 0.0)
    ).astype(BF16)
    for k in range(hid // kb):
        wint[pl.ds(k * kb, kb), :] = dot_nt(eye(kb), wa[:, k * kb : (k + 1) * kb]).astype(BF16)
        w_out[pl.ds(k * kb, kb), :] = dot_nt(eye(kb), woutt[:, k * kb : (k + 1) * kb]).astype(BF16)
    g1[...] = jnp.zeros_like(g1)
    g2[...] = jnp.zeros_like(g2)
    va[...] = jnp.zeros_like(va)
    taps[...] = jnp.zeros_like(taps)
    rc[me] = ca[me]

    def as_f32(flag):
        return jnp.where(flag, 1.0, 0.0).astype(F32)

    def shifted_copies(buf, rbuf, lbuf, cbuf):
        has_up, has_down = as_f32(me_r > 0), as_f32(me_r < n_row - 1)
        has_left, has_right = as_f32(me_c > 0), as_f32(me_c < n_col - 1)
        buf[HALF, pl.ds(0, HALF * cd), :] = rbuf[0].astype(F32)[cd:] * has_up
        buf[HALF, pl.ds((HALF + rows) * cd, HALF * cd), :] = rbuf[1].astype(F32)[: HALF * cd] * has_down
        for side, has in ((0, has_left), (1, has_right)):
            stage[side, 0] = cbuf[0, side].astype(F32)[:cd] * (has * has_up)
            for k in range(n_tiles):
                stage[side, 1 + k] = lbuf[side, k].astype(F32)[:cd] * has
            stage[side, 1 + n_tiles] = cbuf[1, side].astype(F32)[:cd] * (has * has_down)
        lane = lane_iota(cd)

        total = rows + 2 * HALF
        step = next(u for u in (7, 5, 2, 1) if total % u == 0)

        def some_rows(j, carry):
            held = []
            for u in range(step):
                i = j * step + u
                at = i + 32 - HALF
                tile, t = lax.div(at, 32), lax.rem(at, 32)
                where = pl.ds(pl.multiple_of(i * cd, 8), cd)
                held.append((where, t, stage[1, tile], stage[0, tile], buf[HALF, where, :]))
            for where, t, from_right, from_left, x in held:
                halo = jnp.where(
                    lane < 64,
                    pltpu.roll(from_right, lax.rem(LANES - 4 * t, LANES), 1),
                    pltpu.roll(from_left, 124 - 4 * t, 1),
                )
                for s in range(1, HALF + 1):
                    buf[HALF + s, where, :] = pltpu.roll(jnp.where(lane < s, halo, x), LANES - s, 1)
                    buf[HALF - s, where, :] = pltpu.roll(jnp.where(lane >= LANES - s, halo, x), s, 1)
            return carry

        lax.fori_loop(0, total // step, some_rows, 0)

    for copy in halo1:
        copy.wait_recv()

    reach = []
    r = 2
    while r < n_col // 2:
        reach.append(r)
        r *= 2

    def tell(i):
        for step in (reach[i], n_col - reach[i]):
            pl.semaphore_signal(
                ring.at[i],
                inc=1,
                device_id=dict(row=me_r, col=lax.rem(me_c + step, n_col), ch=me),
                device_id_type=MESH,
            )

    if reach:
        tell(0)

    shifted_copies(xs, hrow, hedge, hcorner)

    def conv(buf, base, start, flip):
        def group(g, carry):
            acc = [cb[pl.ds(pl.multiple_of(8 * g, 8), 8), :] if start else jnp.zeros((8, LANES), F32)] * share
            for b in range(KW):
                x = [
                    buf[b, pl.ds(pl.multiple_of((base + i) * cd + 8 * g, 8), 8), :]
                    for i in range(share + 2 * HALF)
                ]
                for a in range(KW):
                    tap = (KW - 1 - a) * KW + KW - 1 - b if flip else a * KW + b
                    w = wb[pl.ds(pl.multiple_of(tap * cd + 8 * g, 8), 8), :]
                    for r in range(share):
                        acc[r] = acc[r] + w * x[r + a]
            for r in range(share):
                cbuf[pl.ds(pl.multiple_of(r * cd + 8 * g, 8), 8), :] = acc[r]
            return carry

        lax.fori_loop(0, cd // 8, group, 0)
        return cbuf[...]

    def mix_copy(q):
        return remote(mb.at[q], rm.at[me], m_s.at[q], m_r.at[me], row=me_r, col=me_c, ch=q)

    def forward(k, carry):
        q = lax.rem(me + 1 + k, n_ch)
        mb[q] = conv(xs, q * share, True, False).astype(BF16)

        @pl.when(k < n_ch - 1)
        def _():
            mix_copy(q).start()

        return carry

    lax.fori_loop(0, n_ch, forward, 0)
    rm[me] = mb[me]

    for k in range(1, n_ch):
        q = lax.rem(me + k, n_ch)
        came(rc, c_s, c_r, q).wait_recv()
        came(rm, m_s, m_r, q).wait_recv()

    if len(reach) > 1:
        pl.semaphore_wait(ring.at[0], 2)
        tell(1)

    px = 2 * LANES
    ones_rows = (lax.broadcasted_iota(jnp.int32, (64, px), 0) < 2).astype(F32).astype(BF16)

    def wide(v):
        return jnp.concatenate([v, v], axis=1)

    def gather(buf, at):
        parts = []
        for q in range(n_ch):
            both = buf[q, at, :].astype(F32)
            parts.append(jnp.concatenate([both[:cd], both[cd:]], axis=1))
        return jnp.concatenate(parts, axis=0)

    def exit_copy(q, k):
        return remote(sb.at[q, k], rb.at[me, k], e_s.at[q, k], e_r.at[me, k], row=me_r, col=me_c, ch=q)

    def fold(v):
        return v[:, :LANES] + v[:, LANES:]

    def chunk(k, carry):
        at = pl.ds(pl.multiple_of(k * pair, 16), pair)
        gain, shift, outb, scale = (wide(vecs[i]) for i in range(4))
        values = gather(rm, at)
        centre = jnp.mean(values, axis=0, keepdims=True)
        away = values - centre
        inv_std = lax.rsqrt(jnp.mean(away * away, axis=0, keepdims=True) + EPSILON)
        normed = away * inv_std
        scaled = (normed * gain + shift).astype(BF16)
        scaled = jnp.concatenate([scaled, ones_rows], axis=0)
        cotan = gather(rc, at)
        cots = (cotan * scale).astype(BF16)
        projected = jnp.zeros((chan, px), F32)
        grad_scaled = jnp.zeros((chan, px), F32)
        for j in range(hid // kb):
            rows_j = pl.ds(j * kb, kb)
            act, slope = gelu_parts(dot(wint[rows_j, :], scaled))
            hidden = act.astype(BF16)
            grad_hidden = (dot(w_out[rows_j, :], cots) * slope).astype(BF16)
            projected = projected + dot(woutt[:, j * kb : (j + 1) * kb], hidden)
            grad_scaled = grad_scaled + dot(w_in[:, j * kb : (j + 1) * kb], grad_hidden)
            g1[rows_j, :] += dot_nt(grad_hidden, scaled)
            g2[rows_j, :] += dot_nt(hidden, cots)
        projected = projected + outb
        branch = scale * projected
        va[0] += fold(cots.astype(F32))
        va[1] += fold(grad_scaled * normed)
        va[2] += fold(grad_scaled)
        va[3] += fold(cotan * projected)
        gn = grad_scaled * gain
        m1 = jnp.mean(gn, axis=0, keepdims=True)
        m2 = jnp.mean(gn * normed, axis=0, keepdims=True)
        gm = (gn - m1 - normed * m2) * inv_std
        for q in range(n_ch):
            for i, v in enumerate((branch, gm)):
                piece = v[q * cd : (q + 1) * cd]
                sb[q, k, pl.ds(i * pair, pair), :] = jnp.concatenate(
                    [piece[:, :LANES], piece[:, LANES:]], axis=0
                ).astype(BF16)
        for d in range(1, n_ch):
            exit_copy(lax.rem(me + d, n_ch), k).start()
        rb[me, k] = sb[me, k]
        return carry

    lax.fori_loop(0, chunks, chunk, 0)

    pair_rows = 2 * hb
    half = lane_iota(pair_rows) < 64
    for par in range(2):
        for r in range(n_row):
            for y in range(0, n_y, 2):
                at = [(2 * (y + i) + par) * hb * n_row + r * hb for i in range(min(2, n_y))]
                a, b = (jnp.concatenate([g[pl.ds(at_i, hb), :] for at_i in at], axis=0) for g in (g1, g2))
                size = hb * len(at)
                b_hi = pltpu.roll(
                    jnp.concatenate([b[:, LANES:], jnp.zeros((size, 2 * LANES - chan), F32)], axis=1), 64, 1
                )
                sc[par, r, pl.ds(y * hb, size), :] = jnp.concatenate(
                    [a[:, :LANES], b[:, :LANES], jnp.where(half[:size], a[:, LANES:], b_hi)], axis=1
                ).astype(BF16)
    p_copy = remote(sc.at[1 - core], rxc, p_s.at[0], p_r.at[0], row=me_r, col=me_c, ch=mate)
    p_copy.start()
    lane_c = lane_iota(chan)
    table = jnp.zeros((chan, LANES), F32)
    for i in range(4):
        table = jnp.where(lane_c == i, jnp.sum(va[i], axis=1, keepdims=True), table)
    for i in range(hid // chan):
        part = pltpu.roll(g1[pl.ds(i * chan, chan), LANES:], LANES - 64 + 4 + i, 1)
        table = jnp.where(lane_c == 4 + i, part, table)
    table = jnp.concatenate([table, jnp.zeros((2 * LANES - chan, LANES), F32)], axis=0)
    sv[...] = table.T[:8]
    pv_copy = remote(sv, rvc, p_s.at[1], p_r.at[1], row=me_r, col=me_c, ch=mate)
    pv_copy.start()

    def x_copies(k):
        r = lax.rem(me_r + k, n_row)
        return (
            remote(sx.at[r], rx.at[me_r], x_s.at[r], x_r.at[me_r], row=r, col=me_c, ch=me),
            remote(svx, rvx.at[me_r], vx_s.at[r], vx_r.at[me_r], row=r, col=me_c, ch=me),
        )

    p_copy.wait_recv()
    pv_copy.wait_recv()
    for r in range(n_row):
        sx[r] = (sc[core, r].astype(F32) + rxc[r].astype(F32)).astype(BF16)
    svx[...] = sv[...] + rvc[...]
    for k in range(1, n_row):
        for copy in x_copies(k):
            copy.start()
    rx[me_r] = sx[me_r]
    rvx[me_r] = svx[...]

    for d in range(1, n_ch):
        q = lax.rem(me + d, n_ch)
        for k in range(chunks):
            came(rb, e_s, e_r, q, k).wait_recv()

    def unpack(q, carry):
        for k in range(chunks):
            at = q * blk + k * pair
            gs[HALF, pl.ds(pl.multiple_of(HALF * cd + at, 8), pair), :] = rb[q, k, pl.ds(pair, pair), :].astype(F32)
        return carry

    lax.fori_loop(0, n_ch, unpack, 0)
    pack_edges(gs.at[HALF], edge2, ends2)
    halo2 = halo_copies(ends2, edge2, hrow2, hedge2, hcorner2, h2_s, h2_r)
    for copy in halo2:
        copy.start()

    def tap_block(q, carry):
        def group(g, c2):
            grad = [
                gs[HALF, pl.ds(pl.multiple_of((HALF + q * share + r) * cd + 8 * g, 8), 8), :]
                for r in range(share)
            ]

            def add(tap, terms):
                while len(terms) > 1:
                    terms = [sum(terms[i : i + 2]) for i in range(0, len(terms), 2)]
                taps[pl.ds(pl.multiple_of(tap * cd + 8 * g, 8), 8), :] += terms[0]

            for b in range(KW):
                x = [
                    xs[b, pl.ds(pl.multiple_of((q * share + i) * cd + 8 * g, 8), 8), :]
                    for i in range(share + 2 * HALF)
                ]
                for a in range(KW):
                    add(a * KW + b, [grad[r] * x[r + a] for r in range(share)])
            add(KW * KW, grad)
            return c2

        return lax.fori_loop(0, cd // 8, group, carry)

    lax.fori_loop(0, n_ch // 2, tap_block, 0)

    for k in range(1, n_row):
        r = lax.rem(me_r + k, n_row)
        remote(rx.at[r], rx.at[r], x_s.at[r], x_r.at[r], row=r, col=me_c, ch=me).wait_recv()
        remote(rvx.at[r], rvx.at[r], vx_s.at[r], vx_r.at[r], row=r, col=me_c, ch=me).wait_recv()
    total, vtotal = rx[0].astype(F32), rvx[0]
    for r in range(1, n_row):
        total = total + rx[r].astype(F32)
        vtotal = vtotal + rvx[r]
    for y in range(n_y):
        sy[y] = total[y * hb : (y + 1) * hb]
    svy[...] = vtotal

    def y_copies(k):
        y = lax.rem(me_y + k, n_y)
        q = 2 * y + core
        return (
            remote(sy.at[y], ry.at[me_y], y_s.at[y], y_r.at[me_y], row=me_r, col=me_c, ch=q),
            remote(svy, rvy.at[me_y], vy_s.at[y], vy_r.at[me_y], row=me_r, col=me_c, ch=q),
        )

    for k in range(1, n_y):
        for copy in y_copies(k):
            copy.start()
    ry[me_y] = sy[me_y]
    rvy[me_y] = svy[...]

    lax.fori_loop(n_ch // 2, n_ch, tap_block, 0)
    lane_d = lane_iota(cd)
    tap_table = jnp.zeros((cd, LANES), F32)
    for t in range(KW * KW + 1):
        col = jnp.sum(taps[pl.ds(t * cd, cd), :], axis=1, keepdims=True)
        tap_table = jnp.where(lane_d == t, col, tap_table)
    for i in range(cd // 8):
        zt[n_gw + 2 + i] = tap_table[8 * i : 8 * i + 8]

    for k in range(1, n_y):
        y = lax.rem(me_y + k, n_y)
        q = 2 * y + core
        remote(ry.at[y], ry.at[y], y_s.at[y], y_r.at[y], row=me_r, col=me_c, ch=q).wait_recv()
        remote(rvy.at[y], rvy.at[y], vy_s.at[y], vy_r.at[y], row=me_r, col=me_c, ch=q).wait_recv()
    total, vtotal = ry[0], rvy[0]
    for y in range(1, n_y):
        total = total + ry[y]
        vtotal = vtotal + rvy[y]
    for i in range(hb // 8):
        for j in range(3):
            zt[3 * i + j] = total[8 * i : 8 * i + 8, j * LANES : (j + 1) * LANES]
    zt[n_gw] = vtotal[:, :LANES]
    zt[n_gw + 1] = vtotal[:, LANES:]

    for i in range(len(reach)):
        if i == len(reach) - 1:
            pl.semaphore_wait(ring.at[i], 2)

    def z_copy(t):
        owner = lax.rem(t, n_col)
        return remote(zt.at[t], rz.at[t, me_c], z_s.at[t], z_r.at[t, me_c], row=me_r, col=owner, ch=me)

    def z_send(t, carry):
        mine = lax.rem(t, n_col) == me_c

        @pl.when(jnp.logical_not(mine))
        def _():
            z_copy(t).start()

        @pl.when(mine)
        def _():
            rz[t, me_c] = zt[t]

        return carry

    lax.fori_loop(0, n_t, z_send, 0)

    for copy in halo2:
        copy.wait_recv()
    shifted_copies(gs, hrow2, hedge2, hcorner2)

    def backward(q, carry):
        rows_q = pl.ds(pl.multiple_of(q * blk, 16), blk)
        gin[rows_q, :] = (conv(gs, q * share, False, True) + ca[q].astype(F32)).astype(BF16)
        for k in range(chunks):
            at = pl.ds(pl.multiple_of(q * blk + k * pair, 16), pair)
            here = xs[HALF, pl.ds(pl.multiple_of(HALF * cd + q * blk + k * pair, 8), pair), :]
            out[at, :] = (here + rb[q, k, pl.ds(0, pair), :].astype(F32)).astype(BF16)
        return carry

    lax.fori_loop(0, n_ch, backward, 0)

    def a_copy(t, c):
        return remote(zs.at[t], zs.at[t], a_s.at[t, c], a_r.at[t], row=me_r, col=c, ch=me)

    def z_own(t, carry):
        @pl.when(lax.rem(t, n_col) == me_c)
        def _():
            def one(d, c2):
                c = lax.rem(me_c + d, n_col)
                remote(rz.at[t, c], rz.at[t, c], z_s.at[t], z_r.at[t, c], row=me_r, col=c, ch=me).wait_recv()
                return c2

            lax.fori_loop(1, n_col, one, 0)
            total = rz[t, 0]
            for c in range(1, n_col):
                total = total + rz[t, c]
            zs[t] = total

            def give(d, c2):
                a_copy(t, lax.rem(me_c + d, n_col)).start()
                return c2

            lax.fori_loop(1, n_col, give, 0)

        return carry

    lax.fori_loop(0, n_t, z_own, 0)

    def f_copy(t, k):
        slot = jnp.where(t < n_gw, t, t - 2)
        r = lax.rem(me_r + k, n_row)
        return remote(zs.at[t], fx.at[me_r, slot], f_s.at[t, r], f_r.at[me_r, t], row=r, col=me_c, ch=me)

    def goes_on(t):
        return (t < n_gw) | (t >= n_gw + 2)

    def hand_on(t):
        @pl.when(goes_on(t))
        def _():
            for k in range(1, n_row):
                f_copy(t, k).start()

    def z_arrived(i, carry):
        t = i

        @pl.when(lax.rem(t, n_col) != me_c)
        def _():
            a_copy(t, lax.rem(t, n_col)).wait_recv()

        hand_on(t)
        return carry

    lax.fori_loop(0, n_t, z_arrived, 0)
    fx[me_r, pl.ds(0, n_gw)] = zs[pl.ds(0, n_gw)]
    fx[me_r, pl.ds(n_gw, cd // 8)] = zs[pl.ds(n_gw + 2, cd // 8)]
    v_out[...] = zs[pl.ds(n_gw, 2)]

    for copy in halo1 + halo2:
        copy.wait_send()
    for k in range(1, n_ch):
        cot_copy(k).wait_send()
        q = lax.rem(me + k, n_ch)
        mix_copy(q).wait_send()
        for j in range(chunks):
            exit_copy(q, j).wait_send()
    p_copy.wait_send()
    pv_copy.wait_send()
    for k in range(1, n_y):
        for copy in y_copies(k):
            copy.wait_send()
    for k in range(1, n_row):
        for copy in x_copies(k):
            copy.wait_send()

    def z_drain(t, carry):
        mine = lax.rem(t, n_col) == me_c

        @pl.when(jnp.logical_not(mine))
        def _():
            z_copy(t).wait_send()

        @pl.when(mine)
        def _():
            def one(d, c2):
                a_copy(t, lax.rem(me_c + d, n_col)).wait_send()
                return c2

            lax.fori_loop(1, n_col, one, 0)

        return carry

    lax.fori_loop(0, n_t, z_drain, 0)

    def f_drain(t, carry):
        @pl.when(goes_on(t))
        def _():
            slot = jnp.where(t < n_gw, t, t - 2)
            for k in range(1, n_row):
                r = lax.rem(me_r + k, n_row)
                there = fx.at[r, slot]
                remote(there, there, f_s.at[t, r], f_r.at[r, t], row=r, col=me_c, ch=me).wait_recv()
                f_copy(t, k).wait_send()

        return carry

    lax.fori_loop(0, n_t, f_drain, 0)


def finish_kernel(dims, fx, v, gi, go, bias, vectors, conv):
    n_row, n_col, n_ch, cd, rows, chan, hid = dims
    hb = hid // n_ch // n_row
    n_gw = hb // 8 * 3
    hs = hid // n_ch
    factor = 1.0 / math.sqrt(rows * n_row * LANES * n_col)
    rest = chan - LANES
    g_in = []
    for r in range(n_row):
        for i in range(hb // 8):
            at = pl.ds(r * hb + 8 * i, 8)
            mixed = fx[r, 3 * i + 2] * factor
            g_in.append(jnp.concatenate([fx[r, 3 * i] * factor, mixed], axis=1))
            go[at, :LANES] = fx[r, 3 * i + 1] * factor
            go[at, LANES:] = mixed[:, 64 : 64 + rest]
    if hs % LANES:
        g_in.append(jnp.zeros((LANES - hs % LANES, 2 * LANES), F32))
    gi[...] = jnp.concatenate(g_in, axis=0).T[:chan, :hs]
    both = jnp.concatenate([v[0], v[1]], axis=1) * factor
    vectors[...] = both[:4, :chan]
    me = lax.axis_index("ch")
    row = jnp.zeros((1, hs), F32)
    flat = jnp.concatenate([both[4 + i : 5 + i, :chan] for i in range(hid // chan)], axis=1)
    for q in range(n_ch):
        row = jnp.where(me == q, flat[:, q * hs : (q + 1) * hs], row)
    bias[...] = row.reshape(hs)
    for i in range(cd // 8):
        total = fx[0, n_gw + i]
        for r in range(1, n_row):
            total = total + fx[r, n_gw + i]
        conv[pl.ds(8 * i, 8), :] = total[:, : KW * KW + 1] * factor


def run_block(dims, *args):
    n_row, n_col, n_ch, cd, rows, chan, hid = dims
    share = rows // n_ch
    chunks = share // 2
    blk = share * cd
    hb = hid // n_ch // n_row
    n_gw = hb // 8 * 3
    n_t = n_gw + 2 + cd // 8
    n_y = n_ch // 2
    pitch = -(-cd // 16) * 16
    n_tiles = rows // 32
    lanes_w = 3 * LANES
    padded = (rows + 2 * HALF) * cd
    vmem = lambda *shape: pltpu.VMEM(shape[:-1], shape[-1])
    dma = lambda *shape: pltpu.SemaphoreType.DMA(shape)
    two = lambda *shape: [dma(*shape), dma(*shape)]
    halo_bufs = [
        vmem(2, n_tiles, pitch, LANES, BF16),
        vmem(2, 4 * cd, LANES, BF16),
        vmem(2, n_tiles, pitch, LANES, BF16),
        vmem(2, 2, pitch, LANES, BF16),
    ]
    scratch = [
        vmem(rows * cd, LANES, F32),
        vmem(n_ch, blk, LANES, BF16),
        vmem(2, 4 * cd, LANES, BF16),
        vmem(2, 4 * cd, LANES, BF16),
        vmem(KW, padded, LANES, F32),
        vmem(KW, padded, LANES, F32),
        vmem(blk, LANES, F32),
        vmem(KW * KW * cd, LANES, F32),
        vmem(cd, LANES, F32),
        vmem(4, chan, LANES, F32),
        *halo_bufs,
        *halo_bufs,
        vmem(2, n_tiles + 2, cd, LANES, F32),
        vmem(n_ch, blk, LANES, BF16),
        vmem(n_ch, blk, LANES, BF16),
        vmem(n_ch, blk, LANES, BF16),
        vmem(n_ch, chunks, 4 * cd, LANES, BF16),
        vmem(n_ch, chunks, 4 * cd, LANES, BF16),
        vmem(chan + 64, hid, BF16),
        vmem(hid, chan + 64, BF16),
        vmem(hid, chan, BF16),
        vmem(hid, chan + 64, F32),
        vmem(hid, chan, F32),
        vmem(4, chan, LANES, F32),
        vmem(2, n_row, n_y * hb, lanes_w, BF16),
        vmem(n_row, n_y * hb, lanes_w, BF16),
        vmem(n_row, n_y * hb, lanes_w, BF16),
        vmem(n_row, n_y * hb, lanes_w, BF16),
        vmem(8, 2 * LANES, F32),
        vmem(8, 2 * LANES, F32),
        vmem(8, 2 * LANES, F32),
        vmem(n_row, 8, 2 * LANES, F32),
        vmem(n_y, hb, lanes_w, F32),
        vmem(n_y, hb, lanes_w, F32),
        vmem(8, 2 * LANES, F32),
        vmem(n_y, 8, 2 * LANES, F32),
        vmem((KW * KW + 1) * cd, LANES, F32),
        vmem(n_t, 8, LANES, F32),
        vmem(n_t, n_col, 8, LANES, F32),
        vmem(n_t, 8, LANES, F32),
        *two(8),
        *two(8),
        *two(n_ch),
        *two(n_ch),
        *two(n_ch, chunks),
        *two(2),
        *two(n_row),
        *two(n_row),
        *two(n_y),
        *two(n_y),
        dma(n_t),
        dma(n_t, n_col),
        dma(n_t, n_col),
        dma(n_t),
        dma(n_t, n_row),
        dma(n_row, n_t),
        pltpu.SemaphoreType.REGULAR((4,)),
    ]
    whole = pl.BlockSpec(memory_space=pltpu.VMEM)
    out, gin, fx, v = pl.pallas_call(
        functools.partial(block_kernel, dims),
        name="convnext_block",
        out_shape=(
            jax.ShapeDtypeStruct((rows * cd, LANES), BF16),
            jax.ShapeDtypeStruct((rows * cd, LANES), BF16),
            jax.ShapeDtypeStruct((n_row, n_gw + cd // 8, 8, LANES), F32),
            jax.ShapeDtypeStruct((2, 8, LANES), F32),
        ),
        in_specs=[whole] * len(args),
        out_specs=(whole,) * 4,
        scratch_shapes=scratch,
        compiler_params=pltpu.CompilerParams(
            collective_id=0, has_side_effects=True, vmem_limit_bytes=56 * 1024 * 1024
        ),
    )(*args)
    hs = hid // n_ch
    small = pl.pallas_call(
        functools.partial(finish_kernel, dims),
        name="finish",
        out_shape=(
            jax.ShapeDtypeStruct((chan, hs), F32),
            jax.ShapeDtypeStruct((hs, chan), F32),
            jax.ShapeDtypeStruct((hs,), F32),
            jax.ShapeDtypeStruct((4, chan), F32),
            jax.ShapeDtypeStruct((cd, KW * KW + 1), F32),
        ),
        in_specs=[whole] * 2,
        out_specs=(whole,) * 5,
    )(fx, v)
    return out, gin, small


def body(
    n_row,
    n_col,
    n_ch,
    features,
    cotangent,
    dw_kernel,
    dw_bias,
    ln_gain,
    ln_bias,
    w_in,
    in_bias,
    w_out,
    out_bias,
    layer_scale,
):
    cd, rows, wide = features.shape
    chan, hid = w_in.shape
    dims = (n_row, n_col, n_ch, cd, rows, chan, hid)
    vectors = (dw_bias, ln_gain, ln_bias, out_bias, layer_scale, in_bias)
    out, gin, small = run_block(dims, features, cotangent, dw_kernel, *vectors, w_in, w_out.T)
    g_in, g_out, g_bias, g_vectors, g_conv = small
    back = lambda v: v.reshape(rows, cd, wide).transpose(1, 0, 2)
    return back(out), back(gin), g_in, g_out, g_bias, g_vectors, g_conv


def solution(mesh):
    ch = P("ch", "row", "col")
    in_specs = (ch, ch, P("ch", None), P("ch")) + (P(),) * 7
    out_specs = (ch, ch, P(None, "ch"), P("ch", None), P("ch"), P(), P("ch", None))
    sizes = (mesh.shape["row"], mesh.shape["col"], mesh.shape["ch"])
    return jax.shard_map(
        functools.partial(body, *sizes), mesh=mesh, in_specs=in_specs, out_specs=out_specs, check_vma=False
    )
```
